32 devices in a mesh: layer: 8 (over z, core), lat: 4 (over y, x).
Axes of the slice: x: 2, y: 2, z: 4, core: 2. Of those that a mesh axis runs over, the one named last changes fastest.
Arguments:
- trace_down: float32 [8, 1024, 128], P('layer', 'lat'), may hold values from -6 to 6
- trace_up: float32 [8, 1024, 128], P('layer', 'lat'), may hold values from -6 to 6
- trans_down: float32 [8, 2, 1024, 4, 128], P('layer', None, 'lat'), may hold values from -0.1875 to 0.1875
- refl_down: float32 [8, 2, 1024, 4, 128], P('layer', None, 'lat'), may hold values from -0.0625 to 0.0625
- trans_up: float32 [8, 2, 1024, 4, 128], P('layer', None, 'lat'), may hold values from -0.1875 to 0.1875
- refl_up: float32 [8, 2, 1024, 4, 128], P('layer', None, 'lat'), may hold values from -0.0625 to 0.0625
- tile_cols: int32 [8, 4, 8, 4], P('layer', None, 'lat'), may hold values from -2 to 9, as said below
- source_down: float32 [1024, 128], P('lat'), may hold values from -6 to 6
- source_up: float32 [1024, 128], P('lat'), may hold values from -6 to 6
- source_layer: int32 [64], replicated, may hold values from 0 to 7
Outputs:
- swept_down: float32 [8, 1024, 128], P('layer', 'lat')
- swept_up: float32 [8, 1024, 128], P('layer', 'lat')
The draws below stay inside these ranges and needn't reach their ends.
Inputs may be any that keep to these rules, and one draw needn't show every extreme that they name: `tile_cols`: for row tile i of each layer and operator, the 4 entries are i - 2, then two different ones of i - 1, i, i + 1 in either order, then i + 2.
All inputs are finite; a program needn't handle non-finite values.
Results may differ from the reference program's by a relative error of at most 0.00015.
Values sent between devices are 32-bit elements; how exact they have to be, the bound alone decides.
A program may use at most 64 MiB of HBM per device.

```python
import jax
import jax.numpy as jnp
from jax import lax

TILE = 128
K_TILES = 4
SRC = 64
TICKS = 5
ROWS = 1024
LAYERS = 8


def draw_tile_cols(key, part):
    row_tiles = ROWS // TILE
    scores = jax.random.randint(key, (LAYERS, 4, row_tiles, 3), 0, 1024)
    scores = scores * 4 + jnp.arange(3, dtype=jnp.int32)
    order = jnp.argsort(scores, axis=-1)
    middle = order[..., :2].astype(jnp.int32) - 1
    lower = jnp.full((LAYERS, 4, row_tiles, 1), -2, jnp.int32)
    upper = jnp.full((LAYERS, 4, row_tiles, 1), 2, jnp.int32)
    offsets = jnp.concatenate([lower, middle, upper], -1)
    base_tiles = jnp.arange(row_tiles, dtype=jnp.int32)[None, None, :, None]
    return (base_tiles + offsets).astype(jnp.int32)


def place_ends(values, own_key, low, high):
    longest = values.shape.index(max(values.shape))
    spots = []
    for shift in (0, 1):
        where = [jax.random.randint(jax.random.fold_in(own_key, axis), (), 0, length) for axis, length in enumerate(values.shape)]
        where[longest] = (where[longest] + shift) % values.shape[longest]
        spots.append(tuple(where))
    return values.at[spots[0]].set(low).at[spots[1]].set(high)


def block_scale(stream_key, shape, pieces, smallest, high):
    level, own = 1.0, jax.random.fold_in(stream_key, 6)
    for axis_at, parts in pieces:
        steps = jnp.exp(jax.random.uniform(jax.random.fold_in(own, axis_at), (parts,), jnp.float32, smallest / len(pieces), high / len(pieces)))
        level = level * jnp.repeat(steps, shape[axis_at] // parts).reshape([-1 if axis == axis_at else 1 for axis in range(len(shape))])
    return level


def gaussian(key, dims, deviation, reach, shards=(), kind=jnp.bfloat16):
    values = jax.random.normal(key, dims, jnp.float32) * deviation
    if len(shards) > 0:
        values = block_scale(key, dims, shards, -0.22, 0.18) * values
    return jnp.clip(values, min=-reach, max=reach).astype(kind)


def setup_inputs(seed: int = 0) -> dict:
    keys = jax.random.split(jax.random.key(seed), 11)
    trace_down = gaussian(keys[0], (LAYERS, ROWS, 2 * SRC), 1.0, 6.0, ((0, 8), (1, 4)), jnp.float32)
    trace_up = gaussian(keys[1], (LAYERS, ROWS, 2 * SRC), 1.0, 6.0, ((0, 8), (1, 4)), jnp.float32)
    trans_down = gaussian(keys[2], (LAYERS, 2, ROWS, K_TILES, TILE), (2 * K_TILES * TILE) ** -0.5, 0.1875, ((0, 8), (2, 4)), jnp.float32)
    refl_down = gaussian(keys[3], (LAYERS, 2, ROWS, K_TILES, TILE), (16 * K_TILES * TILE) ** -0.5, 0.0625, ((0, 8), (2, 4)), jnp.float32)
    trans_up = gaussian(keys[4], (LAYERS, 2, ROWS, K_TILES, TILE), (2 * K_TILES * TILE) ** -0.5, 0.1875, ((0, 8), (2, 4)), jnp.float32)
    refl_up = gaussian(keys[5], (LAYERS, 2, ROWS, K_TILES, TILE), (16 * K_TILES * TILE) ** -0.5, 0.0625, ((0, 8), (2, 4)), jnp.float32)
    tile_cols = draw_tile_cols(jax.random.fold_in(keys[10], 71), 0)
    source_down = gaussian(keys[7], (ROWS, 2 * SRC), 1.0, 6.0, ((0, 4),), jnp.float32)
    source_up = gaussian(keys[8], (ROWS, 2 * SRC), 1.0, 6.0, ((0, 4),), jnp.float32)
    source_layer = place_ends(jax.random.randint(keys[9], (SRC,), 0, LAYERS), jax.random.fold_in(keys[9], 1), 0, LAYERS - 1).astype(jnp.int32)
    return {"trace_down": trace_down, "trace_up": trace_up, "trans_down": trans_down, "refl_down": refl_down, "trans_up": trans_up, "refl_up": refl_up, "tile_cols": tile_cols, "source_down": source_down, "source_up": source_up, "source_layer": source_layer}


def apply_green(green_block, tile_list, trace_rows):
    padded = jnp.pad(trace_rows, ((2 * TILE, 2 * TILE), (0, 0)))
    stacked = padded.reshape(-1, TILE, 2 * SRC)
    picked = stacked[tile_list + 2]
    swapped = jnp.concatenate([-picked[..., SRC:], picked[..., :SRC]], -1)
    row_tiles = ROWS // TILE
    blocks = green_block.reshape(2, row_tiles, TILE, K_TILES, TILE)
    result = jnp.einsum("iakq,ikqc->iac", blocks[0], picked, precision=lax.Precision.HIGHEST)
    result = result + jnp.einsum("iakq,ikqc->iac", blocks[1], swapped, precision=lax.Precision.HIGHEST)
    return result.reshape(ROWS, 2 * SRC)


def reference(trace_down, trace_up, trans_down, refl_down, trans_up, refl_up, tile_cols, source_down, source_up, source_layer):
    empty_trace = jnp.zeros_like(trace_down[:1])
    column_source = jnp.arange(2 * SRC, dtype=jnp.int32) % SRC
    layer_ids = jnp.arange(LAYERS, dtype=jnp.int32)
    source_hits = source_layer[column_source][None, :] == layer_ids[:, None]
    going_down, going_up = trace_down, trace_up
    for sweep in range(TICKS):
        from_above = jnp.concatenate([empty_trace, going_down[:-1]], 0)
        from_below = jnp.concatenate([going_up[1:], empty_trace], 0)

        def one_layer(packed):
            t_down, r_down, t_up, r_up, tile_lists, above, below, hits_row = packed
            new_down = apply_green(t_down, tile_lists[0], above) + apply_green(r_down, tile_lists[1], below)
            new_down = new_down + jnp.where(hits_row[None, :], source_down, 0.0)
            new_up = apply_green(t_up, tile_lists[2], below) + apply_green(r_up, tile_lists[3], above)
            new_up = new_up + jnp.where(hits_row[None, :], source_up, 0.0)
            return new_down, new_up

        going_down, going_up = lax.map(one_layer, (trans_down, refl_down, trans_up, refl_up, tile_cols, from_above, from_below, source_hits))
    return going_down, going_up
```

```python
import functools

import jax
import jax.numpy as jnp
from jax import lax
from jax.experimental import pallas as pl
from jax.experimental.pallas import tpu as pltpu
from jax.sharding import PartitionSpec as P

TICKS = 5
OWN, PARTNER, FAR = 0, 1, 2
OPS = ((0, 3), (1, 2))
MESH = pl.DeviceIdType.MESH


def kernel(
    layers,
    lats,
    sl_ref,
    tc_ref,
    td_ref,
    tu_ref,
    sd_ref,
    su_ref,
    g0_ref,
    g1_ref,
    g2_ref,
    g3_ref,
    od_ref,
    ou_ref,
    gbuf,
    lhs,
    xb,
    acc,
    inj,
    tx,
    rx,
    g_sem,
    tx_sem,
    relay_sem,
    rx_sem,
):
    tile = td_ref.shape[1]
    width = td_ref.shape[2]
    half = width // 2
    quarter = width // 4
    nsrc = sl_ref.shape[0]
    layer = lax.axis_index("layer")
    lat = lax.axis_index("lat")
    par = lax.rem(lat, 2)
    partner = lat + 1 - 2 * par
    relay_to = lat + 2 - 4 * par
    relay_from = lat - 2 + 4 * par
    has_relay_to = jnp.logical_and(relay_to >= 0, relay_to < lats)
    has_far = jnp.logical_and(relay_from >= 0, relay_from < lats)
    has_src = (layer > 0, layer < layers - 1)
    has_dst = (layer < layers - 1, layer > 0)
    dst_layer = (layer + 1, layer - 1)
    sgn = 1 - 2 * par

    g_copies = [
        pltpu.make_async_copy(ref, gbuf.at[op], g_sem.at[op])
        for op, ref in enumerate((g0_ref, g1_ref, g2_ref, g3_ref))
    ]
    for copy in g_copies:
        copy.start()

    barrier = pltpu.get_barrier_semaphore()
    count = jnp.int32(0)
    for d in range(2):
        for other in (lat, partner):

            @pl.when(has_dst[d])
            def _(d=d, other=other):
                pl.semaphore_signal(
                    barrier, inc=1, device_id=(dst_layer[d], other), device_id_type=MESH
                )

        count = count + jnp.where(has_dst[d], 2, 0)

    @pl.when(has_relay_to)
    def _():
        pl.semaphore_signal(barrier, inc=1, device_id=(layer, relay_to), device_id_type=MESH)

    @pl.when(has_far)
    def _():
        pl.semaphore_signal(barrier, inc=1, device_id=(layer, relay_from), device_id_type=MESH)

    count = count + jnp.where(has_relay_to, 1, 0) + jnp.where(has_far, 1, 0)

    lane = lax.broadcasted_iota(jnp.int32, (tile, width), 1)
    first = lax.rem(lane, half) < quarter
    real = lane < half

    def pack(t0, t1):
        return (
            jnp.where(first, t0, pltpu.roll(t1, quarter, 1)),
            jnp.where(first, pltpu.roll(t0, width - quarter, 1), t1),
        )

    def unpack(p0, p1):
        return (
            jnp.where(first, p0, pltpu.roll(p1, quarter, 1)),
            jnp.where(first, pltpu.roll(p0, width - quarter, 1), p1),
        )

    for d, ref in enumerate((td_ref, tu_ref)):
        p0, p1 = pack(ref[0], ref[1])
        tx[0, d] = p0
        tx[1, d] = p1

    def send_copy(slot, g, d, piece):
        return pltpu.make_async_remote_copy(
            src_ref=tx.at[g, d],
            dst_ref=rx.at[slot, g, d, piece],
            send_sem=tx_sem.at[g, d, piece],
            recv_sem=rx_sem.at[slot, g, d, piece],
            device_id=(dst_layer[d], partner if piece == PARTNER else lat),
            device_id_type=MESH,
        )

    def relay_copy(slot, g, d):
        return pltpu.make_async_remote_copy(
            src_ref=rx.at[slot, g, d, PARTNER],
            dst_ref=rx.at[slot, g, d, FAR],
            send_sem=relay_sem.at[g, d],
            recv_sem=rx_sem.at[slot, g, d, FAR],
            device_id=(layer, relay_to),
            device_id_type=MESH,
        )

    def send(slot, g):
        for d in range(2):

            @pl.when(has_dst[d])
            def _(d=d):
                send_copy(slot, g, d, PARTNER).start()
                send_copy(slot, g, d, OWN).start()

    def wait_send(slot, g):
        for d in range(2):

            @pl.when(has_dst[d])
            def _(d=d):
                send_copy(slot, g, d, PARTNER).wait_send()
                send_copy(slot, g, d, OWN).wait_send()

    pl.semaphore_wait(barrier, count)
    for g in range(2):
        send(0, g)

    xb[...] = jnp.zeros_like(xb)
    row = lax.broadcasted_iota(jnp.int32, (8, width), 1)
    row = lax.rem(row, half)
    hits = jnp.zeros((8, width), jnp.float32)
    for s in range(nsrc):
        hit = jnp.where(sl_ref[s] == layer, 1.0, 0.0).astype(jnp.float32)
        hits = jnp.where(row == s, hit, hits)
    hit_row = hits[0:1] > 0.5
    for d, ref in enumerate((sd_ref, su_ref)):
        p0, p1 = pack(jnp.where(hit_row, ref[0], 0.0), jnp.where(hit_row, ref[1], 0.0))
        inj[0, d] = p0
        inj[1, d] = p1

    for copy in g_copies:
        copy.wait()
    for d in range(2):
        for i in range(2):
            ia = i + par - 2 * i * par
            base = ia * (4 * tile)
            for j, op in enumerate(OPS[d]):
                at = lat * 2 + ia
                c1 = (tc_ref[op, ia, 1] - at) * sgn
                c2 = (tc_ref[op, ia, 2] - at) * sgn
                for c in range(2):
                    w1 = gbuf[op, c, pl.ds(base + 1, tile, stride=4), :]
                    w2 = gbuf[op, c, pl.ds(base + 2, tile, stride=4), :]
                    for slot in range(5):
                        if slot == 0:
                            val = gbuf[op, c, pl.ds(base + 3 * par, tile, stride=4), :]
                        elif slot == 4:
                            val = gbuf[op, c, pl.ds(base + 3 - 3 * par, tile, stride=4), :]
                        else:
                            val = jnp.where(c1 == slot - 2, w1, jnp.where(c2 == slot - 2, w2, 0.0))
                        hi = val.astype(jnp.bfloat16)
                        lo = (val - hi.astype(jnp.float32)).astype(jnp.bfloat16)
                        cols = pl.ds(slot * 2 * tile + c * tile, tile)
                        lhs[d, i, pl.ds(j * tile, tile), cols] = hi
                        lhs[d, i, pl.ds((2 + j) * tile, tile), cols] = lo

    def build(slot, g, d, piece, at):
        packed = rx[slot, g, d, piece]
        hi = packed.astype(jnp.bfloat16).astype(jnp.float32)
        lo = packed - hi
        for h in range(2):
            if h == 0:
                x = jnp.where(first, hi, pltpu.roll(lo, quarter, 1))
            else:
                x = jnp.where(first, pltpu.roll(lo, width - quarter, 1), hi)
            other = pltpu.roll(x, half, 1)
            xs = jnp.where(real, -other, other)
            place = (at + h + par - 2 * h * par) * (2 * tile)
            xb[d, pl.ds(place, tile), :] = x.astype(jnp.bfloat16)
            xb[d, pl.ds(place + tile, tile), :] = xs.astype(jnp.bfloat16)

    def wait_recv(slot, g, d, piece):
        if piece == FAR:
            relay_copy(slot, g, d).wait_recv()
        else:
            send_copy(slot, g, d, piece).wait_recv()

    def relay(slot, g):
        for d in range(2):

            @pl.when(has_src[d])
            def _(d=d):
                wait_recv(slot, g, d, PARTNER)

                @pl.when(has_relay_to)
                def _():
                    relay_copy(slot, g, d).start()

    def products(slots_of, tiles_of):
        sums = [[None, None], [None, None]]
        for i in range(2):
            s0, s1 = slots_of[i]
            e0 = tiles_of[i]
            for d in range(2):
                y = jnp.dot(
                    lhs[d, i, :, pl.ds(s0 * 2 * tile, (s1 - s0) * 2 * tile)],
                    xb[d, pl.ds(e0 * 2 * tile, (s1 - s0) * 2 * tile), :],
                    preferred_element_type=jnp.float32,
                )
                for j in range(2):
                    part = y[j * tile : (j + 1) * tile] + y[(2 + j) * tile : (3 + j) * tile]
                    sums[i][j] = part if d == 0 else sums[i][j] + part
        return sums

    def near(slot, g):
        for d in range(2):

            @pl.when(has_src[d])
            def _(d=d):
                wait_recv(slot, g, d, OWN)
                build(slot, g, d, OWN, 2)
                build(slot, g, d, PARTNER, 4)

        sums = products(((2, 5), (1, 5)), (2, 2))
        for i in range(2):
            for j in range(2):
                acc[i, j] = sums[i][j]

    swap = jnp.logical_xor(first, par == 1)

    def far(tick, slot, g):
        for d in range(2):

            @pl.when(jnp.logical_and(has_src[d], has_far))
            def _(d=d):
                wait_recv(slot, g, d, FAR)
                build(slot, g, d, FAR, 0)

        sums = products(((0, 2), (0, 1)), (0, 1))
        for d in range(2):

            @pl.when(jnp.logical_and(has_src[d], has_relay_to))
            def _(d=d):
                relay_copy(slot, g, d).wait_send()

        wait_send(slot, g)
        for j in range(2):
            s0 = sums[0][j] + acc[0, j]
            s1 = sums[1][j] + acc[1, j]
            ya = jnp.where(swap, s0, s1)
            other = jnp.where(first, pltpu.roll(s0, width - quarter, 1), pltpu.roll(s0, quarter, 1))
            other1 = jnp.where(first, pltpu.roll(s1, width - quarter, 1), pltpu.roll(s1, quarter, 1))
            tx[g, j] = ya + jnp.where(swap, other, other1) + inj[g, j]

        @pl.when(tick < TICKS - 1)
        def _():
            send(1 - slot, g)

    relay(0, 0)

    def tick_body(tick, carry):
        slot = lax.rem(tick, 2)
        near(slot, 0)
        relay(slot, 1)
        far(tick, slot, 0)
        near(slot, 1)

        @pl.when(tick < TICKS - 1)
        def _():
            relay(1 - slot, 0)

        far(tick, slot, 1)
        return carry

    lax.fori_loop(0, TICKS, tick_body, 0)
    for d, ref in enumerate((od_ref, ou_ref)):
        t0, t1 = unpack(tx[0, d], tx[1, d])
        ref[0] = t0
        ref[1] = t1


def on_device(
    layers,
    lats,
    trace_down,
    trace_up,
    trans_down,
    refl_down,
    trans_up,
    refl_up,
    tile_cols,
    source_down,
    source_up,
    source_layer,
):
    tile = trans_down.shape[-1]
    rows, width = trace_down.shape[1], trace_down.shape[2]
    row_tiles = rows // tile
    assert row_tiles == 2 and lats % 2 == 0
    strip = (row_tiles, tile, width)
    vmem = pl.BlockSpec(memory_space=pltpu.VMEM)
    smem = pl.BlockSpec(memory_space=pltpu.SMEM)
    hbm = pl.BlockSpec(memory_space=pl.ANY)
    greens = [g.reshape(2, rows * 4, tile) for g in (trans_down, refl_down, trans_up, refl_up)]
    out = jax.ShapeDtypeStruct(strip, jnp.float32)
    down, up = pl.pallas_call(
        functools.partial(kernel, layers, lats),
        out_shape=(out, out),
        in_specs=[smem, smem, vmem, vmem, vmem, vmem, hbm, hbm, hbm, hbm],
        out_specs=(vmem, vmem),
        scratch_shapes=[
            pltpu.VMEM((4, 2, rows * 4, tile), jnp.float32),
            pltpu.VMEM((2, 2, 4 * tile, 10 * tile), jnp.bfloat16),
            pltpu.VMEM((2, 12 * tile, width), jnp.bfloat16),
            pltpu.VMEM((2, 2, tile, width), jnp.float32),
            pltpu.VMEM((2, 2, tile, width), jnp.float32),
            pltpu.VMEM((2, 2, tile, width), jnp.float32),
            pltpu.VMEM((2, 2, 2, 3, tile, width), jnp.float32),
            pltpu.SemaphoreType.DMA((4,)),
            pltpu.SemaphoreType.DMA((2, 2, 2)),
            pltpu.SemaphoreType.DMA((2, 2)),
            pltpu.SemaphoreType.DMA((2, 2, 2, 3)),
        ],
        compiler_params=pltpu.CompilerParams(
            collective_id=0, has_side_effects=True, vmem_limit_bytes=40 * 1024 * 1024
        ),
    )(
        source_layer,
        tile_cols[0],
        trace_down.reshape(strip),
        trace_up.reshape(strip),
        source_down.reshape(strip),
        source_up.reshape(strip),
        *greens,
    )
    return (down.reshape(1, rows, width), up.reshape(1, rows, width))


def solution(mesh):
    in_specs = (
        P("layer", "lat", None),
        P("layer", "lat", None),
        P("layer", None, "lat", None, None),
        P("layer", None, "lat", None, None),
        P("layer", None, "lat", None, None),
        P("layer", None, "lat", None, None),
        P("layer", None, "lat", None),
        P("lat", None),
        P("lat", None),
        P(),
    )
    out_specs = (P("layer", "lat", None), P("layer", "lat", None))
    return jax.shard_map(
        functools.partial(on_device, mesh.shape["layer"], mesh.shape["lat"]),
        mesh=mesh,
        in_specs=in_specs,
        out_specs=out_specs,
        check_vma=False,
    )
```

```python
import functools

import jax
import jax.numpy as jnp
from jax import lax
from jax.experimental import pallas as pl
from jax.experimental.pallas import tpu as pltpu
from jax.sharding import PartitionSpec as P

TICKS = 5
OWN, PARTNER, FAR = 0, 1, 2
CHUNKS = 2
OPS = ((0, 3), (1, 2))
MESH = pl.DeviceIdType.MESH


def kernel(
    layers,
    lats,
    sl_ref,
    tc_ref,
    td_ref,
    tu_ref,
    sd_ref,
    su_ref,
    g0_ref,
    g1_ref,
    g2_ref,
    g3_ref,
    od_ref,
    ou_ref,
    raw,
    gbuf,
    lhs,
    xb,
    acc,
    inj,
    tx,
    rx,
    raw_sem,
    g_sem,
    tx_sem,
    relay_sem,
    rx_sem,
):
    tile = td_ref.shape[1]
    width = td_ref.shape[2]
    half = width // 2
    quarter = width // 4
    nsrc = sl_ref.shape[0]
    layer = lax.axis_index("layer")
    lat = lax.axis_index("lat")
    par = lax.rem(lat, 2)
    partner = lat + 1 - 2 * par
    relay_to = lat + 2 - 4 * par
    relay_from = lat - 2 + 4 * par
    has_relay_to = jnp.logical_and(relay_to >= 0, relay_to < lats)
    has_far = jnp.logical_and(relay_from >= 0, relay_from < lats)
    has_src = (layer > 0, layer < layers - 1)
    has_dst = (layer < layers - 1, layer > 0)
    dst_layer = (layer + 1, layer - 1)
    sgn = 1 - 2 * par

    raw_copies = [
        pltpu.make_async_copy(ref, raw.at[n], raw_sem.at[n])
        for n, ref in enumerate((td_ref, tu_ref, sd_ref, su_ref))
    ]
    for copy in raw_copies:
        copy.start()
    g_copies = [
        pltpu.make_async_copy(ref, gbuf.at[op], g_sem.at[op])
        for op, ref in enumerate((g0_ref, g1_ref, g2_ref, g3_ref))
    ]
    for copy in g_copies:
        copy.start()

    barrier = pltpu.get_barrier_semaphore()
    count = jnp.int32(0)
    for d in range(2):
        for other in (lat, partner):

            @pl.when(has_dst[d])
            def _(d=d, other=other):
                pl.semaphore_signal(
                    barrier, inc=1, device_id=(dst_layer[d], other), device_id_type=MESH
                )

        count = count + jnp.where(has_dst[d], 2, 0)

    @pl.when(has_relay_to)
    def _():
        pl.semaphore_signal(barrier, inc=1, device_id=(layer, relay_to), device_id_type=MESH)

    @pl.when(has_far)
    def _():
        pl.semaphore_signal(barrier, inc=1, device_id=(layer, relay_from), device_id_type=MESH)

    count = count + jnp.where(has_relay_to, 1, 0) + jnp.where(has_far, 1, 0)

    lane = lax.broadcasted_iota(jnp.int32, (tile, width), 1)
    first = lax.rem(lane, half) < quarter
    real = lane < half

    def pack(t0, t1):
        return (
            jnp.where(first, t0, pltpu.roll(t1, quarter, 1)),
            jnp.where(first, pltpu.roll(t0, width - quarter, 1), t1),
        )

    def unpack(p0, p1):
        return (
            jnp.where(first, p0, pltpu.roll(p1, quarter, 1)),
            jnp.where(first, pltpu.roll(p0, width - quarter, 1), p1),
        )

    for d in range(2):
        raw_copies[d].wait()
        p0, p1 = pack(raw[d, 0], raw[d, 1])
        tx[0, d] = p0
        tx[1, d] = p1

    chunk_rows = tile // CHUNKS

    def send_copy(slot, g, d, piece, n):
        rows = pl.ds(n * chunk_rows, chunk_rows)
        return pltpu.make_async_remote_copy(
            src_ref=tx.at[g, d, rows],
            dst_ref=rx.at[slot, g, d, piece, rows],
            send_sem=tx_sem.at[g, d, piece, n],
            recv_sem=rx_sem.at[slot, g, d, piece, n],
            device_id=(dst_layer[d], partner if piece == PARTNER else lat),
            device_id_type=MESH,
        )

    def relay_copy(slot, g, d, n):
        rows = pl.ds(n * chunk_rows, chunk_rows)
        return pltpu.make_async_remote_copy(
            src_ref=rx.at[slot, g, d, PARTNER, rows],
            dst_ref=rx.at[slot, g, d, FAR, rows],
            send_sem=relay_sem.at[g, d, n],
            recv_sem=rx_sem.at[slot, g, d, FAR, n],
            device_id=(layer, relay_to),
            device_id_type=MESH,
        )

    def send(slot, g):
        for d in range(2):

            @pl.when(has_dst[d])
            def _(d=d):
                for piece in (PARTNER, OWN):
                    for n in range(CHUNKS):
                        send_copy(slot, g, d, piece, n).start()

    def wait_send(slot, g):
        for d in range(2):

            @pl.when(has_dst[d])
            def _(d=d):
                for piece in (PARTNER, OWN):
                    for n in range(CHUNKS):
                        send_copy(slot, g, d, piece, n).wait_send()

    pl.semaphore_wait(barrier, count)
    for g in range(2):
        send(0, g)

    xb[...] = jnp.zeros_like(xb)
    row = lax.broadcasted_iota(jnp.int32, (8, width), 1)
    row = lax.rem(row, half)
    hits = jnp.zeros((8, width), jnp.float32)
    for s in range(nsrc):
        hit = jnp.where(sl_ref[s] == layer, 1.0, 0.0).astype(jnp.float32)
        hits = jnp.where(row == s, hit, hits)
    hit_row = hits[0:1] > 0.5
    for d in range(2):
        raw_copies[2 + d].wait()
        p0, p1 = pack(
            jnp.where(hit_row, raw[2 + d, 0], 0.0), jnp.where(hit_row, raw[2 + d, 1], 0.0)
        )
        inj[0, d] = p0
        inj[1, d] = p1

    for copy in g_copies:
        copy.wait()
    for d in range(2):
        for i in range(2):
            ia = i + par - 2 * i * par
            base = ia * (4 * tile)
            for j, op in enumerate(OPS[d]):
                at = lat * 2 + ia
                c1 = (tc_ref[op, ia, 1] - at) * sgn
                c2 = (tc_ref[op, ia, 2] - at) * sgn
                for c in range(2):
                    w1 = gbuf[op, c, pl.ds(base + 1, tile, stride=4), :]
                    w2 = gbuf[op, c, pl.ds(base + 2, tile, stride=4), :]
                    for slot in range(5):
                        if slot == 0:
                            val = gbuf[op, c, pl.ds(base + 3 * par, tile, stride=4), :]
                        elif slot == 4:
                            val = gbuf[op, c, pl.ds(base + 3 - 3 * par, tile, stride=4), :]
                        else:
                            val = jnp.where(c1 == slot - 2, w1, jnp.where(c2 == slot - 2, w2, 0.0))
                        hi = val.astype(jnp.bfloat16)
                        lo = (val - hi.astype(jnp.float32)).astype(jnp.bfloat16)
                        cols = pl.ds(slot * 2 * tile + c * tile, tile)
                        lhs[d, i, pl.ds(j * tile, tile), cols] = hi
                        lhs[d, i, pl.ds((2 + j) * tile, tile), cols] = lo

    def build(slot, g, d, piece, at):
        packed = rx[slot, g, d, piece]
        hi = packed.astype(jnp.bfloat16).astype(jnp.float32)
        lo = packed - hi
        for h in range(2):
            if h == 0:
                x = jnp.where(first, hi, pltpu.roll(lo, quarter, 1))
            else:
                x = jnp.where(first, pltpu.roll(lo, width - quarter, 1), hi)
            other = pltpu.roll(x, half, 1)
            xs = jnp.where(real, -other, other)
            place = (at + h + par - 2 * h * par) * (2 * tile)
            xb[d, pl.ds(place, tile), :] = x.astype(jnp.bfloat16)
            xb[d, pl.ds(place + tile, tile), :] = xs.astype(jnp.bfloat16)

    def wait_recv(slot, g, d, piece):
        for n in range(CHUNKS):
            if piece == FAR:
                relay_copy(slot, g, d, n).wait_recv()
            else:
                send_copy(slot, g, d, piece, n).wait_recv()

    def relay(slot, g):
        for d in range(2):

            @pl.when(has_src[d])
            def _(d=d):
                for n in range(CHUNKS):
                    send_copy(slot, g, d, PARTNER, n).wait_recv()

                    @pl.when(has_relay_to)
                    def _(n=n):
                        relay_copy(slot, g, d, n).start()

    def product(d, i, slot0, slot1, e0):
        y = jnp.dot(
            lhs[d, i, :, pl.ds(slot0 * 2 * tile, (slot1 - slot0) * 2 * tile)],
            xb[d, pl.ds(e0 * 2 * tile, (slot1 - slot0) * 2 * tile), :],
            preferred_element_type=jnp.float32,
        )
        return [y[j * tile : (j + 1) * tile] + y[(2 + j) * tile : (3 + j) * tile] for j in range(2)]

    def near(slot, g):
        for d in range(2):

            @pl.when(has_src[d])
            def _(d=d):
                wait_recv(slot, g, d, OWN)
                build(slot, g, d, OWN, 2)
                build(slot, g, d, PARTNER, 4)

        for i in range(2):
            parts = [product(d, i, 2 - i, 5, 2) for d in range(2)]
            for j in range(2):
                acc[i, j] = parts[0][j] + parts[1][j]

    swap = jnp.logical_xor(first, par == 1)

    def far(tick, slot, g):
        for d in range(2):

            @pl.when(jnp.logical_and(has_src[d], has_far))
            def _(d=d):
                wait_recv(slot, g, d, FAR)
                build(slot, g, d, FAR, 0)
                for i in range(2):
                    part = product(d, i, 0, 2 - i, i)
                    for j in range(2):
                        acc[i, j] += part[j]

        for d in range(2):

            @pl.when(jnp.logical_and(has_src[d], has_relay_to))
            def _(d=d):
                for n in range(CHUNKS):
                    relay_copy(slot, g, d, n).wait_send()

        wait_send(slot, g)
        for j in range(2):
            s0, s1 = acc[0, j], acc[1, j]
            other0 = jnp.where(first, pltpu.roll(s0, width - quarter, 1), pltpu.roll(s0, quarter, 1))
            other1 = jnp.where(first, pltpu.roll(s1, width - quarter, 1), pltpu.roll(s1, quarter, 1))
            tx[g, j] = jnp.where(swap, s0 + other0, s1 + other1) + inj[g, j]

        @pl.when(tick < TICKS - 1)
        def _():
            send(1 - slot, g)

    def tick_body(tick, carry):
        slot = lax.rem(tick, 2)
        for g in range(2):
            relay(slot, g)
            near(slot, g)
            far(tick, slot, g)
        return carry

    lax.fori_loop(0, TICKS, tick_body, 0)
    for d, ref in enumerate((od_ref, ou_ref)):
        t0, t1 = unpack(tx[0, d], tx[1, d])
        ref[0] = t0
        ref[1] = t1


def on_device(
    layers,
    lats,
    trace_down,
    trace_up,
    trans_down,
    refl_down,
    trans_up,
    refl_up,
    tile_cols,
    source_down,
    source_up,
    source_layer,
):
    tile = trans_down.shape[-1]
    rows, width = trace_down.shape[1], trace_down.shape[2]
    row_tiles = rows // tile
    assert row_tiles == 2 and lats % 2 == 0
    strip = (row_tiles, tile, width)
    vmem = pl.BlockSpec(memory_space=pltpu.VMEM)
    smem = pl.BlockSpec(memory_space=pltpu.SMEM)
    hbm = pl.BlockSpec(memory_space=pltpu.HBM)
    greens = [g.reshape(2, rows * 4, tile) for g in (trans_down, refl_down, trans_up, refl_up)]
    out = jax.ShapeDtypeStruct(strip, jnp.float32)
    down, up = pl.pallas_call(
        functools.partial(kernel, layers, lats),
        out_shape=(out, out),
        in_specs=[smem, smem] + [hbm] * 8,
        out_specs=(vmem, vmem),
        scratch_shapes=[
            pltpu.VMEM((4,) + strip, jnp.float32),
            pltpu.VMEM((4, 2, rows * 4, tile), jnp.float32),
            pltpu.VMEM((2, 2, 4 * tile, 10 * tile), jnp.bfloat16),
            pltpu.VMEM((2, 12 * tile, width), jnp.bfloat16),
            pltpu.VMEM((2, 2, tile, width), jnp.float32),
            pltpu.VMEM((2, 2, tile, width), jnp.float32),
            pltpu.VMEM((2, 2, tile, width), jnp.float32),
            pltpu.VMEM((2, 2, 2, 3, tile, width), jnp.float32),
            pltpu.SemaphoreType.DMA((4,)),
            pltpu.SemaphoreType.DMA((4,)),
            pltpu.SemaphoreType.DMA((2, 2, 2, CHUNKS)),
            pltpu.SemaphoreType.DMA((2, 2, CHUNKS)),
            pltpu.SemaphoreType.DMA((2, 2, 2, 3, CHUNKS)),
        ],
        compiler_params=pltpu.CompilerParams(
            collective_id=0, has_side_effects=True
        ),
    )(
        source_layer,
        tile_cols[0],
        trace_down.reshape(strip),
        trace_up.reshape(strip),
        source_down.reshape(strip),
        source_up.reshape(strip),
        *greens,
    )
    return (down.reshape(1, rows, width), up.reshape(1, rows, width))


def solution(mesh):
    in_specs = (
        P("layer", "lat", None),
        P("layer", "lat", None),
        P("layer", None, "lat", None, None),
        P("layer", None, "lat", None, None),
        P("layer", None, "lat", None, None),
        P("layer", None, "lat", None, None),
        P("layer", None, "lat", None),
        P("lat", None),
        P("lat", None),
        P(),
    )
    out_specs = (P("layer", "lat", None), P("layer", "lat", None))
    return jax.shard_map(
        functools.partial(on_device, mesh.shape["layer"], mesh.shape["lat"]),
        mesh=mesh,
        in_specs=in_specs,
        out_specs=out_specs,
        check_vma=False,
    )
```
